128 devices in a mesh: grp: 2 (over core), voc: 64 (over z, y, x).
Axes of the slice: x: 4, y: 4, z: 4, core: 2. Of those that a mesh axis runs over, the one named last changes fastest.
Arguments:
- expert_hidden: bfloat16 [512, 8192], P(('grp', 'voc')), may hold values from -6 to 6
- expert_gain: float32 [8192], replicated, may hold values from 0.25 to 1.75
- expert_head: bfloat16 [128256, 8192], P('voc', 'grp'), may hold values from -0.2541165 to 0.2541165
- amateur_hidden: bfloat16 [512, 2048], P(('grp', 'voc')), may hold values from -6 to 6
- mlp_gain: float32 [2048], replicated, may hold values from 0.25 to 1.75
- gate_weight: bfloat16 [2048, 8192], P(None, 'voc'), may hold values from -0.125 to 0.125
- up_weight: bfloat16 [2048, 8192], P(None, 'voc'), may hold values from -0.125 to 0.125
- down_weight: bfloat16 [8192, 2048], P('voc'), may hold values from -0.25 to 0.25
- amateur_gain: float32 [2048], replicated, may hold values from 0.25 to 1.75
- amateur_embed: bfloat16 [128256, 2048], P('voc', 'grp'), may hold values from -0.508233 to 0.508233
- plausible: int32 [512, 256], P('grp'), may hold values from 0 to 128255
- targets: int32 [512], P('grp'), may hold values from 0 to 128255
Outputs:
- contrast: float32 [512, 256], P(('grp', 'voc'))
- entropy: float32 [512], P(('grp', 'voc'))
- target_score: float32 [512], P(('grp', 'voc'))
The draws below stay inside these ranges and needn't reach their ends.
All inputs are finite; a program needn't handle non-finite values.
Results may differ from the reference program's by a relative error of at most 0.0063.
Values may be sent and summed in bfloat16 or wider, within the bound.
A program may use at most 192 MiB of HBM per device.

```python
import math
import jax
import jax.numpy as jnp
import numpy as np
from jax import lax

DE = 8192
DA = 2048
FF = 8192
V = 128256
K = 256
ROWS = 512


def vocab_rows(key, count, width):
    base = jnp.clip(jax.random.normal(jax.random.fold_in(key, 11), (count, width), jnp.float32), -3.0, 3.0)
    spread = jnp.exp(jax.random.uniform(jax.random.fold_in(key, 12), (count, 1), jnp.float32, minval=0.0, maxval=math.log(10.0)))
    ramp = 1.0 + 0.5 * jnp.arange(count, dtype=jnp.float32)[:, None] / count
    return base * spread * ramp * (0.5 / math.sqrt(width))


def draw_expert_head(key, part):
    return vocab_rows(jax.random.fold_in(key, 101), V, DE).astype(jnp.bfloat16)


def draw_amateur_embed(key, part):
    return vocab_rows(jax.random.fold_in(key, 202), V, DA).astype(jnp.bfloat16)


def set_ends(array, rng, smallest, largest):
    longest = array.shape.index(max(array.shape))
    spots = []
    for shift in (0, 1):
        where = [jax.random.randint(jax.random.fold_in(rng, axis), (), 0, length) for axis, length in enumerate(array.shape)]
        where[longest] = (where[longest] + shift) % array.shape[longest]
        spots.append(tuple(where))
    return array.at[spots[0]].set(smallest).at[spots[1]].set(largest)


def steps_of(stream_key, dims, cuts, least, top_value):
    level, own = 1.0, jax.random.fold_in(stream_key, 6)
    for dim, shards_of in cuts:
        draws = jnp.exp(jax.random.uniform(jax.random.fold_in(own, dim), (shards_of,), jnp.float32, least / len(cuts), top_value / len(cuts)))
        level = level * jnp.repeat(draws, dims[dim] // shards_of).reshape([-1 if axis == dim else 1 for axis in range(len(dims))])
    return level


def wide_ids(own_key, extent, number_of, skew):
    portions = [min(1 << octave, number_of + 1 - (1 << octave)) * (1 << 20) // math.isqrt((1 << octave) ** skew) + 1 for octave in range((number_of + 1).bit_length()) if 1 << octave <= number_of]
    scale = 1 + sum(portions) // (1 << 30)
    listing = np.cumsum(np.array([max(1, weight // scale) for weight in portions]))
    ticket = jax.random.randint(jax.random.fold_in(own_key, 1), extent, 0, int(listing[len(portions) - 1]))
    start = jnp.left_shift(1, jnp.searchsorted(jnp.asarray(listing, jnp.int32), ticket, side="right").astype(jnp.int32))
    standing = start - 1 + jax.random.randint(jax.random.fold_in(own_key, 4), extent, 0, 1 << 30) % jnp.minimum(start, number_of + 1 - start)
    return jax.random.permutation(jax.random.fold_in(own_key, 2), number_of)[standing].astype(jnp.int32)


def centred(key, dims, deviation, bound, split=(), kind=jnp.bfloat16):
    entries = jax.random.normal(key, dims, jnp.float32) * deviation
    if len(split) > 0:
        entries = steps_of(key, dims, split, -0.22, 0.18) * entries
    return jnp.clip(entries, min=-bound, max=bound).astype(kind)


def setup_inputs(seed: int = 0) -> dict:
    splits = jax.random.split(jax.random.key(seed), 13)
    return {
        "expert_hidden": centred(splits[0], (ROWS, DE), 1.0, 6.0, ((0, 128),)),
        "expert_gain": jnp.clip(1.0 + 0.15 * jax.random.normal(splits[1], (DE,), jnp.float32), 0.25, 1.75),
        "expert_head": draw_expert_head(jax.random.fold_in(splits[12], 71), 0),
        "amateur_hidden": centred(splits[3], (ROWS, DA), 1.0, 6.0, ((0, 128),)),
        "mlp_gain": jnp.clip(1.0 + 0.15 * jax.random.normal(splits[4], (DA,), jnp.float32), 0.25, 1.75),
        "gate_weight": centred(splits[5], (DA, FF), DA ** -0.5, 0.125, ((1, 64),)),
        "up_weight": centred(splits[6], (DA, FF), DA ** -0.5, 0.125, ((1, 64),)),
        "down_weight": centred(splits[7], (FF, DA), (FF // 16) ** -0.5, 0.25, ((0, 64),)),
        "amateur_gain": jnp.clip(1.0 + 0.15 * jax.random.normal(splits[8], (DA,), jnp.float32), 0.25, 1.75),
        "amateur_embed": draw_amateur_embed(jax.random.fold_in(splits[12], 71), 0),
        "plausible": set_ends(jax.random.randint(splits[10], (ROWS, K), 0, V), jax.random.fold_in(splits[10], 1), 0, V - 1).astype(jnp.int32),
        "targets": set_ends(wide_ids(splits[11], (ROWS,), V, 2), jax.random.fold_in(splits[11], 3), 0, V - 1).astype(jnp.int32),
    }


EPS = 1e-05
BETA = 0.5

def rms_scale(values, gain):
    return values * jax.lax.rsqrt(lax.optimization_barrier(jnp.mean(values * values, axis=-1, keepdims=True)) + EPS) * gain

def reference(expert_hidden, expert_gain, expert_head, amateur_hidden, mlp_gain, gate_weight, up_weight, down_weight, amateur_gain, amateur_embed, plausible, targets):
    expert_rows = rms_scale(expert_hidden.astype(jnp.float32), expert_gain).astype(jnp.bfloat16)
    expert_logits = jnp.dot(expert_rows, expert_head.T, preferred_element_type=jnp.float32)
    resid = amateur_hidden.astype(jnp.float32)
    mlp_in = rms_scale(resid, mlp_gain).astype(jnp.bfloat16)
    gate = jnp.dot(mlp_in, gate_weight, preferred_element_type=jnp.float32)
    upper = jnp.dot(mlp_in, up_weight, preferred_element_type=jnp.float32)
    inner = (jax.nn.silu(gate) * upper).astype(jnp.bfloat16)
    branch = jnp.dot(inner, down_weight, preferred_element_type=jnp.float32)
    amateur_rows = rms_scale(resid + branch, amateur_gain).astype(jnp.bfloat16)
    amateur_logits = jnp.dot(amateur_rows, amateur_embed.T, preferred_element_type=jnp.float32)
    lse_e = jnp.log(lax.optimization_barrier(jnp.sum(jnp.exp(expert_logits), axis=1)))
    lse_a = jnp.log(lax.optimization_barrier(jnp.sum(jnp.exp(amateur_logits), axis=1)))
    pick_e = jnp.take_along_axis(expert_logits, plausible, axis=1)
    pick_a = jnp.take_along_axis(amateur_logits, plausible, axis=1)
    scores = pick_e - lse_e[:, None] - BETA * (pick_a - lse_a[:, None])
    contrast = scores - jnp.log(lax.optimization_barrier(jnp.sum(jnp.exp(scores), axis=1, keepdims=True)))
    entropy = -lax.optimization_barrier(jnp.sum(jnp.exp(contrast) * contrast, axis=1))
    targ_e = jnp.take_along_axis(expert_logits, targets[:, None], axis=1)[:, 0]
    targ_a = jnp.take_along_axis(amateur_logits, targets[:, None], axis=1)[:, 0]
    target_score = targ_e - lse_e - BETA * (targ_a - lse_a)
    return (contrast, entropy, target_score)
```

```python
import functools

import jax
import jax.numpy as jnp
from jax import lax
from jax.experimental import pallas as pl
from jax.experimental.pallas import tpu as pltpu
from jax.sharding import PartitionSpec as P

EPS = 1e-05
BETA = 0.5
MESH = pl.DeviceIdType.MESH
TILE = 256
LANES = 128


def copy_for_each(x, axis):
    devices = lax.axis_size(axis)
    return lax.all_to_all(jnp.broadcast_to(x[None], (devices, *x.shape)), axis, 0, 0, tiled=True)


def in_blocks(x, dim, devices):
    before, after = (x.shape[:dim], x.shape[dim + 1 :])
    return jnp.moveaxis(x.reshape(*before, devices, -1, *after), dim, 0)


def sum_at_owner(x, axis, dim):
    pieces = in_blocks(x, dim, lax.axis_size(axis))
    arrived = lax.all_to_all(pieces, axis, split_axis=0, concat_axis=0, tiled=True)
    return arrived.sum(axis=0)


def rms_scale(values, gain):
    return values * lax.rsqrt(jnp.mean(values * values, axis=-1, keepdims=True) + EPS) * gain


def score_kernel(
    x_ref, a_ref, plaus_ref, targ_ref, head_hbm, embed_hbm, out_ref,
    head, embed, part_e, part_a, got_e, got_a, picked, sums,
    load_sem, send_sem, recv_sem,
):
    grp, voc = lax.axis_index("grp"), lax.axis_index("voc")
    peer = 1 - grp
    shard = head_hbm.shape[0]
    padded = head.shape[0]
    tiles = padded // TILE
    rows = plaus_ref.shape[0]
    whole = shard // 16 * 16

    head[whole:, :] = jnp.zeros((padded - whole, head.shape[1]), head.dtype)
    embed[whole:, :] = jnp.zeros((padded - whole, embed.shape[1]), embed.dtype)
    aligned = shard // 8 * 8
    loads = []
    for m, (src, dst) in enumerate(((head_hbm, head), (embed_hbm, embed))):
        spans = [(0, aligned)] + [(aligned, shard - aligned)] * (shard > aligned)
        loads.append([
            pltpu.make_async_copy(src.at[pl.ds(*s), :], dst.at[pl.ds(*s), :], load_sem.at[m, i])
            for i, s in enumerate(spans)
        ])
        for load in loads[m]:
            load.start()

    barrier = pltpu.get_barrier_semaphore()
    pl.semaphore_signal(barrier, inc=1, device_id={"grp": peer}, device_id_type=MESH)
    pl.semaphore_wait(barrier, 1)

    def exchange(m, j):
        part, got = ((part_e, got_e), (part_a, got_a))[m]
        return pltpu.make_async_remote_copy(
            src_ref=part.at[j, pl.ds(peer * rows, rows), :],
            dst_ref=got.at[j],
            send_sem=send_sem.at[m, j],
            recv_sem=recv_sem.at[m, j],
            device_id={"grp": peer},
            device_id_type=MESH,
        )

    def partial(m, left, weight, part):
        @pl.loop(0, tiles)
        def _(j):
            block = weight[pl.ds(pl.multiple_of(j * TILE, TILE), TILE), :]
            part[j] = lax.dot_general(
                left[...], block, (((1,), (1,)), ((), ())), preferred_element_type=jnp.float32
            )
            exchange(m, j).start()

    for load in loads[0]:
        load.wait()
    partial(0, x_ref, head, part_e)
    for load in loads[1]:
        load.wait()
    partial(1, a_ref, embed, part_a)

    picked[...] = jnp.zeros_like(picked)
    sums[...] = jnp.zeros_like(sums)
    target = targ_ref[...] - voc * shard
    lane = lax.broadcasted_iota(jnp.int32, (rows, LANES), 1)
    slots = plaus_ref.shape[1] // LANES
    own = pl.ds(grp * rows, rows)

    @pl.loop(0, tiles)
    def _(j):
        exchange(0, j).wait()
        exchange(1, j).wait()
        for half in range(TILE // LANES):
            at = pl.ds(half * LANES, LANES)
            expert = part_e[j, own, at] + got_e[j, :, at]
            amateur = part_a[j, own, at] + got_a[j, :, at]
            chunk = j * (TILE // LANES) + half
            column = chunk * LANES + lane
            valid = column < shard
            sums[0] += jnp.where(valid, jnp.exp(expert), 0.0)
            sums[1] += jnp.where(valid, jnp.exp(amateur), 0.0)
            both = jnp.where(valid, expert - BETA * amateur, 0.0)
            sums[2] += jnp.where(column == target, both, 0.0)
            for s in range(slots):
                local = plaus_ref[:, s * LANES : (s + 1) * LANES] - voc * shard
                found = jnp.take_along_axis(both, local & (LANES - 1), axis=1)
                here = (local >> 7 == chunk) & (local < shard)
                picked[s] = jnp.where(here, found, picked[s])

    for s in range(slots):
        out_ref[:, s * LANES : (s + 1) * LANES] = picked[s]
    total_e = jnp.sum(sums[0], axis=1, keepdims=True)
    total_a = jnp.sum(sums[1], axis=1, keepdims=True)
    at_target = jnp.sum(sums[2], axis=1, keepdims=True)
    tail = jnp.where(lane == 0, at_target, jnp.where(lane == 1, total_e, total_a))
    out_ref[:, slots * LANES :] = tail


def scores_of(x, a, plausible, targets, head, embed):
    rows, slots = plausible.shape
    padded = pl.cdiv(head.shape[0], TILE) * TILE
    tiles = padded // TILE
    vmem = pl.BlockSpec(memory_space=pltpu.VMEM)
    hbm = pl.BlockSpec(memory_space=pl.ANY)
    return pl.pallas_call(
        score_kernel,
        out_shape=jax.ShapeDtypeStruct((rows, slots + LANES), jnp.float32),
        in_specs=[vmem] * 4 + [hbm] * 2,
        out_specs=vmem,
        scratch_shapes=[
            pltpu.VMEM((padded, head.shape[1]), head.dtype),
            pltpu.VMEM((padded, embed.shape[1]), embed.dtype),
            pltpu.VMEM((tiles, 2 * rows, TILE), jnp.float32),
            pltpu.VMEM((tiles, 2 * rows, TILE), jnp.float32),
            pltpu.VMEM((tiles, rows, TILE), jnp.float32),
            pltpu.VMEM((tiles, rows, TILE), jnp.float32),
            pltpu.VMEM((slots // LANES, rows, LANES), jnp.float32),
            pltpu.VMEM((3, rows, LANES), jnp.float32),
            pltpu.SemaphoreType.DMA((2, 2)),
            pltpu.SemaphoreType.DMA((2, tiles)),
            pltpu.SemaphoreType.DMA((2, tiles)),
        ],
        compiler_params=pltpu.CompilerParams(
            collective_id=0, has_side_effects=True, vmem_limit_bytes=56 << 20
        ),
    )(x, a, plausible, targets, head, embed)


def half_width(rows):
    count, width = rows.shape
    halves = rows.reshape(count, 2, width // 2).swapaxes(0, 1)
    return lax.all_to_all(halves, "grp", 0, 0, tiled=True)


def all_rows(gathered):
    devices, groups, count, width = gathered.shape
    return gathered.swapaxes(0, 1).reshape(groups * devices * count, width)


def on_device(
    expert_hidden,
    expert_gain,
    expert_head,
    amateur_hidden,
    mlp_gain,
    gate_weight,
    up_weight,
    down_weight,
    amateur_gain,
    amateur_embed,
    plausible,
    targets,
):
    normed = rms_scale(expert_hidden.astype(jnp.float32), expert_gain).astype(jnp.bfloat16)
    expert_rows = all_rows(lax.all_gather(half_width(normed), "voc", axis=0))
    resid = copy_for_each(amateur_hidden, "voc").reshape(-1, amateur_hidden.shape[1])
    mlp_in = rms_scale(resid.astype(jnp.float32), mlp_gain).astype(jnp.bfloat16)
    gate = jnp.dot(mlp_in, gate_weight, preferred_element_type=jnp.float32)
    upper = jnp.dot(mlp_in, up_weight, preferred_element_type=jnp.float32)
    inner = (jax.nn.silu(gate) * upper).astype(jnp.bfloat16)
    own_branch = sum_at_owner(
        jnp.dot(inner, down_weight, preferred_element_type=jnp.float32), "voc", 0
    )
    own_final = rms_scale(amateur_hidden.astype(jnp.float32) + own_branch, amateur_gain).astype(
        jnp.bfloat16
    )
    amateur_rows = all_rows(copy_for_each(half_width(own_final), "voc"))
    found = scores_of(
        expert_rows, amateur_rows, plausible, targets[:, None], expert_head, amateur_embed
    )
    total = sum_at_owner(found, "voc", 0)
    slots = plausible.shape[1]
    lse_e = jnp.log(total[:, slots + 1])
    lse_a = jnp.log(total[:, slots + 2])
    shift = lse_e - BETA * lse_a
    scores = total[:, :slots] - shift[:, None]
    target_score = total[:, slots] - shift
    contrast = scores - jnp.log(jnp.sum(jnp.exp(scores), axis=1, keepdims=True))
    entropy = -jnp.sum(jnp.exp(contrast) * contrast, axis=1)
    return (contrast, entropy, target_score)


def solution(mesh):
    in_specs = (
        P(("grp", "voc"), None),
        P(),
        P("voc", "grp"),
        P(("grp", "voc"), None),
        P(),
        P(None, "voc"),
        P(None, "voc"),
        P("voc", None),
        P(),
        P("voc", "grp"),
        P("grp", None),
        P("grp"),
    )
    out_specs = (P(("grp", "voc"), None), P(("grp", "voc")), P(("grp", "voc")))
    return jax.shard_map(
        on_device, mesh=mesh, in_specs=in_specs, out_specs=out_specs, check_vma=False
    )
```

```python
import functools

import jax
import jax.numpy as jnp
from jax import lax
from jax.experimental import pallas as pl
from jax.experimental.pallas import tpu as pltpu
from jax.sharding import PartitionSpec as P

EPS = 1e-05
BETA = 0.5
MESH = pl.DeviceIdType.MESH
TILE = 256
LANES = 128
RING = 4
AXES = 3
OWN = 4


def rms_scale(values, gain):
    return values * lax.rsqrt(jnp.mean(values * values, axis=-1, keepdims=True) + EPS) * gain


def thirds(width):
    lanes, spans, at = width // LANES, [], 0
    for p in range(AXES):
        count = (lanes + p) // AXES * LANES
        spans.append((at, count))
        at += count
    return spans


def order_of(p):
    return [(p + s) % AXES for s in range(AXES)]


def slots_shape(p, s, columns):
    left = [axis for axis in range(AXES) if axis not in order_of(p)[: s + 1]]
    lead = [RING for axis in left if axis < 2]
    return (RING, *lead, OWN * RING if 2 in left else OWN, columns)


def reduce_buffers(width, dtype):
    spans = thirds(width)
    got = [[pltpu.VMEM(slots_shape(p, s, n), dtype) for p, (_, n) in enumerate(spans)] for s in range(3)]
    sums = [[pltpu.VMEM(slots_shape(p, s, n)[1:], dtype) for p, (_, n) in enumerate(spans)] for s in range(2)]
    sems = [pltpu.SemaphoreType.DMA((3, AXES, RING))] * 2
    return [got, sums, *sems]


class Torus:
    def __init__(self):
        self.grp, voc = lax.axis_index("grp"), lax.axis_index("voc")
        self.voc = voc
        self.me = (voc // (RING * RING), voc // RING % RING, voc % RING)
        self.sent = []

    def shifted(self, axis, d):
        place = [(c + d) % RING if a == axis else c for a, c in enumerate(self.me)]
        return (place[0] * RING + place[1]) * RING + place[2]

    def copy(self, src, dst, send, recv, grp, voc):
        made = pltpu.make_async_remote_copy(
            src_ref=src, dst_ref=dst, send_sem=send, recv_sem=recv,
            device_id={"grp": grp, "voc": voc}, device_id_type=MESH,
        )
        made.start()
        self.sent.append(made)
        return made

    def local(self, src, dst, sem):
        made = pltpu.make_async_copy(src, dst, sem)
        made.start()
        return made

    def greet(self):
        barrier = pltpu.get_barrier_semaphore()
        others = [(1 - self.grp, self.voc)]
        for axis in range(AXES):
            for d in range(1, RING):
                for grp in (self.grp, 1 - self.grp):
                    others.append((grp, self.shifted(axis, d)))
        for grp, voc in others:
            pl.semaphore_signal(
                barrier, inc=1, device_id={"grp": grp, "voc": voc}, device_id_type=MESH
            )
        pl.semaphore_wait(barrier, len(others))

    def gather_first(self, src, dst, sems, halves):
        send, recv = sems
        width = dst.shape[-1]
        z, y, x = self.me
        copies = []
        for p, (at, n) in enumerate(thirds(width)):
            lead = self.grp if halves else 0
            place = dst.at[lead, z, y, pl.ds(x * OWN, OWN), pl.ds(at, n)]
            for other in range(2 if halves else 1):
                grp = 1 - self.grp if other else self.grp
                start = pl.multiple_of(grp * width + at, LANES) if halves else at
                piece = src.at[:, pl.ds(start, n)]
                for d in range(RING):
                    k = other * RING + d
                    if k == 0:
                        copies.append(self.local(piece, place, recv.at[0, p, 0]))
                    else:
                        copies.append(
                            self.copy(
                                piece, place, send.at[0, p, k], recv.at[0, p, k],
                                grp, self.shifted(p, d),
                            )
                        )
        return copies

    def gather_next(self, s, dst, sems):
        send, recv = sems
        z, y, x = self.me
        copies = []
        for p, (at, n) in enumerate(thirds(dst.shape[-1])):
            order = order_of(p)
            done = order[:s]
            block = dst.at[
                :,
                pl.ds(0, RING) if 0 in done else pl.ds(z, 1),
                pl.ds(0, RING) if 1 in done else pl.ds(y, 1),
                pl.ds(0, RING * OWN) if 2 in done else pl.ds(x * OWN, OWN),
                pl.ds(at, n),
            ]
            for d in range(1, RING):
                copies.append(
                    self.copy(
                        block, block, send.at[s, p, d], recv.at[s, p, d],
                        self.grp, self.shifted(order[s], d),
                    )
                )
        return copies

    def reduce_stage(self, s, src, buffers, width):
        got, sums, send, recv = buffers
        copies = []
        for p, (at, n) in enumerate(thirds(width)):
            order = order_of(p)
            axis = order[s]
            left = [a for a in range(AXES) if a not in order[:s]]
            source = src if s == 0 else sums[s - 1][p]
            for d in range(RING):
                c = (self.me[axis] + d) % RING
                index = [c if a == axis else slice(None) for a in left if a < 2]
                index.append(pl.ds(c * OWN, OWN) if axis == 2 else slice(None))
                index.append(pl.ds(at, n) if s == 0 else slice(None))
                piece = source.at[tuple(index)]
                slot = got[s][p].at[self.me[axis]]
                if d == 0:
                    copies.append(self.local(piece, slot, recv.at[s, p, 0]))
                else:
                    copies.append(
                        self.copy(
                            piece, slot, send.at[s, p, d], recv.at[s, p, d],
                            self.grp, self.shifted(axis, d),
                        )
                    )
        return copies

    def reduce_scatter(self, src, buffers, result, meanwhile=None):
        got, sums, _, _ = buffers
        width = result.shape[-1]
        for s in range(3):
            copies = self.reduce_stage(s, src, buffers, width)
            if meanwhile is not None:
                meanwhile(s)
            arrived(copies)
            for p, (at, n) in enumerate(thirds(width)):
                total = got[s][p][0].astype(jnp.float32)
                for k in range(1, RING):
                    total += got[s][p][k].astype(jnp.float32)
                if s < 2:
                    sums[s][p][...] = total.astype(sums[s][p].dtype)
                else:
                    result[:, at : at + n] = total


def arrived(copies):
    for made in copies:
        if made.is_remote:
            made.wait_recv()
        else:
            made.wait()


def whole_kernel(
    hidden_ref, gain_ref, resid_ref, mlp_gain_ref, last_gain_ref, plaus_ref, targ_ref,
    gate_hbm, up_hbm, down_hbm, head_hbm, embed_hbm,
    out_ref, stat_ref,
    gate, up, down, head, embed, load_sem,
    normed, x_all, x_sems, h_all, h_sems, last, a_all, a_sems,
    branch, branch_buffers, summed,
    part_e, part_a, got_e, got_a, picked, sums, swap_send, swap_recv,
    found, found_buffers, total_ref,
):
    torus = Torus()
    grp, voc = torus.grp, torus.voc
    peer = 1 - grp
    shard = head_hbm.shape[0]
    padded = head.shape[0]
    tiles = padded // TILE
    rows = plaus_ref.shape[0]

    weights = [
        torus.local(src, dst, load_sem.at[i, 0])
        for i, (src, dst) in enumerate(((gate_hbm, gate), (up_hbm, up), (down_hbm, down)))
    ]
    torus.greet()

    copies_h = torus.gather_first(resid_ref, h_all, h_sems, False)
    normed[...] = rms_scale(hidden_ref[...].astype(jnp.float32), gain_ref[...]).astype(normed.dtype)
    copies_x = torus.gather_first(normed, x_all, x_sems, True)

    whole = shard // 16 * 16
    aligned = shard // 8 * 8
    loads = []
    for m, (src, dst) in enumerate(((head_hbm, head), (embed_hbm, embed))):
        dst[whole:, :] = jnp.zeros((padded - whole, dst.shape[1]), dst.dtype)
        spans = [(0, aligned)] + [(aligned, shard - aligned)] * (shard > aligned)
        loads.append([
            torus.local(src.at[pl.ds(*span), :], dst.at[pl.ds(*span), :], load_sem.at[3 + m, i])
            for i, span in enumerate(spans)
        ])

    arrived(copies_h)
    copies_h = torus.gather_next(1, h_all, h_sems)
    arrived(copies_x)
    copies_x = torus.gather_next(1, x_all, x_sems)
    arrived(copies_h)
    copies_h = torus.gather_next(2, h_all, h_sems)
    arrived(copies_x)
    copies_x = torus.gather_next(2, x_all, x_sems)
    arrived(weights)
    arrived(copies_h)

    hidden = h_all[...].reshape(rows, h_all.shape[-1]).astype(jnp.float32)
    mlp_in = rms_scale(hidden, mlp_gain_ref[...]).astype(jnp.bfloat16)
    gated = jnp.dot(mlp_in, gate[...], preferred_element_type=jnp.float32)
    upper = jnp.dot(mlp_in, up[...], preferred_element_type=jnp.float32)
    inner = (gated / (1.0 + jnp.exp(-gated)) * upper).astype(jnp.bfloat16)
    partial = jnp.dot(inner, down[...], preferred_element_type=jnp.float32)
    branch[...] = partial.astype(branch.dtype).reshape(branch.shape)
    torus.reduce_scatter(branch, branch_buffers, summed)

    final = resid_ref[...].astype(jnp.float32) + summed[...]
    last[...] = rms_scale(final, last_gain_ref[...]).astype(last.dtype)

    def exchange(m, j):
        part, got = ((part_e, got_e), (part_a, got_a))[m]
        return pltpu.make_async_remote_copy(
            src_ref=part.at[j, pl.ds(peer * rows, rows), :],
            dst_ref=got.at[j],
            send_sem=swap_send.at[m, j],
            recv_sem=swap_recv.at[m, j],
            device_id={"grp": peer, "voc": voc},
            device_id_type=MESH,
        )

    def partial_logits(m, first, stop):
        left, weight, part = ((x_all, head, part_e), (a_all, embed, part_a))[m]

        @pl.loop(first, stop)
        def _(j):
            block = weight[pl.ds(pl.multiple_of(j * TILE, TILE), TILE), :]
            part[j] = lax.dot_general(
                left[...].reshape(2 * rows, left.shape[-1]), block,
                (((1,), (1,)), ((), ())), preferred_element_type=jnp.float32,
            )
            exchange(m, j).start()

    copies_a = torus.gather_first(last, a_all, a_sems, True)
    arrived(copies_x)
    arrived(loads[0])
    cut = (0, tiles // 4, tiles // 2, tiles)
    for s in range(1, 3):
        partial_logits(0, cut[s - 1], cut[s])
        arrived(copies_a)
        copies_a = torus.gather_next(s, a_all, a_sems)
    partial_logits(0, cut[2], cut[3])
    arrived(copies_a)
    arrived(loads[1])
    partial_logits(1, 0, tiles)

    picked[...] = jnp.zeros_like(picked)
    sums[...] = jnp.zeros_like(sums)
    target = targ_ref[...] - voc * shard
    lane = lax.broadcasted_iota(jnp.int32, (rows, LANES), 1)
    slots = plaus_ref.shape[1] // LANES
    own = pl.ds(grp * rows, rows)

    @pl.loop(0, tiles)
    def _(j):
        exchange(0, j).wait()
        exchange(1, j).wait()
        for half in range(TILE // LANES):
            at = pl.ds(half * LANES, LANES)
            expert = part_e[j, own, at] + got_e[j, :, at]
            amateur = part_a[j, own, at] + got_a[j, :, at]
            chunk = j * (TILE // LANES) + half
            column = chunk * LANES + lane
            valid = column < shard
            sums[0] += jnp.where(valid, jnp.exp(expert), 0.0)
            sums[1] += jnp.where(valid, jnp.exp(amateur), 0.0)
            both = jnp.where(valid, expert - BETA * amateur, 0.0)
            sums[2] += jnp.where(column == target, both, 0.0)
            for s in range(slots):
                local = plaus_ref[:, s * LANES : (s + 1) * LANES] - voc * shard
                taken = jnp.take_along_axis(both, local & (LANES - 1), axis=1)
                here = (local >> 7 == chunk) & (local < shard)
                picked[s] = jnp.where(here, taken, picked[s])

    place = (*found.shape[:3], LANES)
    for s in range(slots):
        found[:, :, :, s * LANES : (s + 1) * LANES] = picked[s].reshape(place)
    total_e = jnp.sum(sums[0], axis=1, keepdims=True)
    total_a = jnp.sum(sums[1], axis=1, keepdims=True)
    at_target = jnp.sum(sums[2], axis=1, keepdims=True)
    tail = jnp.where(lane == 0, at_target, jnp.where(lane == 1, total_e, total_a))
    found[:, :, :, slots * LANES :] = tail.reshape(place)

    torus.reduce_scatter(found, found_buffers, total_ref)
    count = slots * LANES
    total = total_ref[...]
    shift = jnp.log(total[:, count + 1 : count + 2]) - BETA * jnp.log(total[:, count + 2 : count + 3])
    scores = total[:, :count] - shift
    contrast = scores - jnp.log(jnp.sum(jnp.exp(scores), axis=1, keepdims=True))
    out_ref[...] = contrast
    entropy = -jnp.sum(jnp.exp(contrast) * contrast, axis=1, keepdims=True)
    lane = lax.broadcasted_iota(jnp.int32, stat_ref.shape, 1)
    stat_ref[...] = jnp.where(lane == 0, entropy, total[:, count : count + 1] - shift)
    for made in torus.sent:
        made.wait_send()


def on_device(
    expert_hidden,
    expert_gain,
    expert_head,
    amateur_hidden,
    mlp_gain,
    gate_weight,
    up_weight,
    down_weight,
    amateur_gain,
    amateur_embed,
    plausible,
    targets,
):
    rows, slots = plausible.shape
    shard, wide = expert_head.shape
    narrow = amateur_embed.shape[1]
    width, units = gate_weight.shape
    padded = pl.cdiv(shard, TILE) * TILE
    tiles = padded // TILE
    bf16, f32 = jnp.bfloat16, jnp.float32
    vmem = pl.BlockSpec(memory_space=pltpu.VMEM)
    hbm = pl.BlockSpec(memory_space=pl.ANY)
    dma = pltpu.SemaphoreType.DMA
    stage_sems = [dma((3, AXES, 2 * RING))] * 2
    torus_rows = (RING, RING, RING * OWN)
    out, stats = pl.pallas_call(
        whole_kernel,
        out_shape=(
            jax.ShapeDtypeStruct((OWN, slots), f32),
            jax.ShapeDtypeStruct((OWN, LANES), f32),
        ),
        in_specs=[vmem] * 7 + [hbm] * 5,
        out_specs=(vmem, vmem),
        scratch_shapes=[
            pltpu.VMEM((width, units), bf16),
            pltpu.VMEM((width, units), bf16),
            pltpu.VMEM((units, width), bf16),
            pltpu.VMEM((padded, wide), bf16),
            pltpu.VMEM((padded, narrow), bf16),
            dma((5, 2)),
            pltpu.VMEM((OWN, 2 * wide), bf16),
            pltpu.VMEM((2, *torus_rows, wide), bf16),
            stage_sems,
            pltpu.VMEM((1, *torus_rows, width), bf16),
            stage_sems,
            pltpu.VMEM((OWN, width), bf16),
            pltpu.VMEM((2, *torus_rows, narrow), bf16),
            stage_sems,
            pltpu.VMEM((*torus_rows, width), bf16),
            reduce_buffers(width, bf16),
            pltpu.VMEM((OWN, width), f32),
            pltpu.VMEM((tiles, 2 * rows, TILE), f32),
            pltpu.VMEM((tiles, 2 * rows, TILE), f32),
            pltpu.VMEM((tiles, rows, TILE), f32),
            pltpu.VMEM((tiles, rows, TILE), f32),
            pltpu.VMEM((slots // LANES, rows, LANES), f32),
            pltpu.VMEM((3, rows, LANES), f32),
            dma((2, tiles)),
            dma((2, tiles)),
            pltpu.VMEM((*torus_rows, slots + LANES), f32),
            reduce_buffers(slots + LANES, f32),
            pltpu.VMEM((OWN, slots + LANES), f32),
        ],
        compiler_params=pltpu.CompilerParams(
            collective_id=0, has_side_effects=True, vmem_limit_bytes=60 << 20
        ),
    )(
        expert_hidden, expert_gain[None], amateur_hidden, mlp_gain[None], amateur_gain[None],
        plausible, targets[:, None], gate_weight, up_weight, down_weight, expert_head, amateur_embed,
    )
    return (out, stats[:, 0], stats[:, 1])


def solution(mesh):
    in_specs = (
        P(("grp", "voc"), None),
        P(),
        P("voc", "grp"),
        P(("grp", "voc"), None),
        P(),
        P(None, "voc"),
        P(None, "voc"),
        P("voc", None),
        P(),
        P("voc", "grp"),
        P("grp", None),
        P("grp"),
    )
    out_specs = (P(("grp", "voc"), None), P(("grp", "voc")), P(("grp", "voc")))
    return jax.shard_map(
        on_device, mesh=mesh, in_specs=in_specs, out_specs=out_specs, check_vma=False
    )
```

```python
import functools

import jax
import jax.numpy as jnp
from jax import lax
from jax.experimental import pallas as pl
from jax.experimental.pallas import tpu as pltpu
from jax.sharding import PartitionSpec as P

EPS = 1e-05
BETA = 0.5
MESH = pl.DeviceIdType.MESH
TILE = 512
LANES = 128
RING = 4
AXES = 3
OWN = 4


def rms_scale(values, gain):
    return values * lax.rsqrt(jnp.mean(values * values, axis=-1, keepdims=True) + EPS) * gain


def thirds(width):
    lanes, spans, at = width // LANES, [], 0
    for p in range(AXES):
        count = (lanes + p) // AXES * LANES
        spans.append((at, count))
        at += count
    return spans


def order_of(p):
    return [(p + s) % AXES for s in range(AXES)]


def slots_shape(p, s, columns):
    left = [axis for axis in range(AXES) if axis not in order_of(p)[: s + 1]]
    lead = [RING for axis in left if axis < 2]
    return (RING, *lead, OWN * RING if 2 in left else OWN, columns)


def reduce_buffers(width, dtype):
    spans = thirds(width)
    got = [[pltpu.VMEM(slots_shape(p, s, n), dtype) for p, (_, n) in enumerate(spans)] for s in range(3)]
    sums = [[pltpu.VMEM(slots_shape(p, s, n)[1:], dtype) for p, (_, n) in enumerate(spans)] for s in range(2)]
    sems = [pltpu.SemaphoreType.DMA((3, AXES, RING))] * 2
    return [got, sums, *sems]


class Torus:
    def __init__(self):
        self.grp, voc = lax.axis_index("grp"), lax.axis_index("voc")
        self.voc = voc
        self.me = (voc // (RING * RING), voc // RING % RING, voc % RING)
        self.sent = []

    def shifted(self, axis, d):
        place = [(c + d) % RING if a == axis else c for a, c in enumerate(self.me)]
        return (place[0] * RING + place[1]) * RING + place[2]

    def copy(self, src, dst, send, recv, grp, voc):
        made = pltpu.make_async_remote_copy(
            src_ref=src, dst_ref=dst, send_sem=send, recv_sem=recv,
            device_id={"grp": grp, "voc": voc}, device_id_type=MESH,
        )
        made.start()
        self.sent.append(made)
        return made

    def local(self, src, dst, sem):
        made = pltpu.make_async_copy(src, dst, sem)
        made.start()
        return made

    def greet(self):
        barrier = pltpu.get_barrier_semaphore()
        others = [(1 - self.grp, self.voc)]
        for axis in range(AXES):
            for d in range(1, RING):
                for grp in (self.grp, 1 - self.grp):
                    others.append((grp, self.shifted(axis, d)))
        for grp, voc in others:
            pl.semaphore_signal(
                barrier, inc=1, device_id={"grp": grp, "voc": voc}, device_id_type=MESH
            )
        pl.semaphore_wait(barrier, len(others))

    def drain(self, keep=0):
        count = len(self.sent) - keep
        for made in self.sent[:count]:
            made.wait_send()
        del self.sent[:count]

    def gather_first(self, src, dst, sems, halves):
        send, recv = sems
        width = dst.shape[-1]
        z, y, x = self.me
        copies = []
        for p, (at, n) in enumerate(thirds(width)):
            lead = self.grp if halves else 0
            place = dst.at[lead, z, y, pl.ds(x * OWN, OWN), pl.ds(at, n)]
            for other in range(2 if halves else 1):
                grp = 1 - self.grp if other else self.grp
                start = pl.multiple_of(grp * width + at, LANES) if halves else at
                piece = src.at[:, pl.ds(start, n)]
                for d in range(RING):
                    k = other * RING + d
                    if k == 0:
                        copies.append(self.local(piece, place, recv.at[0, p, 0]))
                    else:
                        copies.append(
                            self.copy(
                                piece, place, send.at[0, p, k], recv.at[0, p, k],
                                grp, self.shifted(p, d),
                            )
                        )
        return copies

    def gather_next(self, s, dst, sems):
        send, recv = sems
        z, y, x = self.me
        copies = []
        for p, (at, n) in enumerate(thirds(dst.shape[-1])):
            order = order_of(p)
            done = order[:s]
            block = dst.at[
                :,
                pl.ds(0, RING) if 0 in done else pl.ds(z, 1),
                pl.ds(0, RING) if 1 in done else pl.ds(y, 1),
                pl.ds(0, RING * OWN) if 2 in done else pl.ds(x * OWN, OWN),
                pl.ds(at, n),
            ]
            for d in range(1, RING):
                copies.append(
                    self.copy(
                        block, block, send.at[s, p, d], recv.at[s, p, d],
                        self.grp, self.shifted(order[s], d),
                    )
                )
        return copies

    def gather_last(self, dst, sems, step, before=None):
        send, recv = sems
        copies = []
        for p, (at, n) in enumerate(thirds(dst.shape[-1])):
            axis = order_of(p)[2]

            def block(lead, c):
                index = [pl.ds(0, RING), pl.ds(0, RING), pl.ds(0, RING * OWN)]
                index[axis] = pl.ds(c * OWN, OWN) if axis == 2 else pl.ds(c, 1)
                return dst.at[(lead, *index, pl.ds(at, n))]

            for way, d in enumerate((1, RING - 1)):
                if step == 0:
                    k, piece = d, block(slice(None), self.me[axis])
                else:
                    before[2 * p + way].wait_recv()
                    k, piece = RING + way, block(pl.ds(way, 1), (self.me[axis] + RING - d) % RING)
                copies.append(
                    self.copy(piece, piece, send.at[2, p, k], recv.at[2, p, k], self.grp, self.shifted(axis, d))
                )
        return copies

    def reduce_stage(self, s, src, buffers, width):
        got, sums, send, recv = buffers
        copies = []
        for p, (at, n) in enumerate(thirds(width)):
            order = order_of(p)
            axis = order[s]
            left = [a for a in range(AXES) if a not in order[:s]]
            source = src if s == 0 else sums[s - 1][p]
            for d in range(RING):
                c = (self.me[axis] + d) % RING
                index = [c if a == axis else slice(None) for a in left if a < 2]
                index.append(pl.ds(c * OWN, OWN) if axis == 2 else slice(None))
                index.append(pl.ds(at, n) if s == 0 else slice(None))
                piece = source.at[tuple(index)]
                slot = got[s][p].at[self.me[axis]]
                if d == 0:
                    copies.append(self.local(piece, slot, recv.at[s, p, 0]))
                else:
                    copies.append(
                        self.copy(
                            piece, slot, send.at[s, p, d], recv.at[s, p, d],
                            self.grp, self.shifted(axis, d),
                        )
                    )
        return copies

    def reduce_scatter(self, src, buffers, result, meanwhile=None):
        got, sums, _, _ = buffers
        width = result.shape[-1]
        for s in range(3):
            copies = self.reduce_stage(s, src, buffers, width)
            if meanwhile is not None:
                meanwhile(s)
            arrived(copies)
            for p, (at, n) in enumerate(thirds(width)):
                total = got[s][p][0].astype(jnp.float32)
                for k in range(1, RING):
                    total += got[s][p][k].astype(jnp.float32)
                if s < 2:
                    sums[s][p][...] = total.astype(sums[s][p].dtype)
                else:
                    result[:, at : at + n] = total


def arrived(copies):
    for made in copies:
        if made.is_remote:
            made.wait_recv()
        else:
            made.wait()


def whole_kernel(
    hidden_ref, gain_ref, resid_ref, mlp_gain_ref, last_gain_ref, plaus_ref, targ_ref,
    gate_hbm, up_hbm, down_hbm, head_hbm, embed_hbm,
    out_ref, stat_ref,
    gate, up, down, head, embed, load_sem,
    normed, x_all, x_sems, h_all, h_sems, last, a_all, a_sems,
    branch, branch_buffers, summed,
    part_e, part_a, got_e, got_a, picked, sums, swap_send, swap_recv,
    found, found_buffers, total_ref,
):
    torus = Torus()
    grp, voc = torus.grp, torus.voc
    peer = 1 - grp
    shard = head_hbm.shape[0]
    padded = head.shape[0]
    tiles = padded // TILE
    rows = plaus_ref.shape[0]

    weights = [
        torus.local(src, dst, load_sem.at[i, 0])
        for i, (src, dst) in enumerate(((gate_hbm, gate), (up_hbm, up), (down_hbm, down)))
    ]
    torus.greet()

    copies_h = torus.gather_first(resid_ref, h_all, h_sems, False)
    normed[...] = rms_scale(hidden_ref[...].astype(jnp.float32), gain_ref[...]).astype(normed.dtype)
    copies_x = torus.gather_first(normed, x_all, x_sems, True)

    whole = shard // 16 * 16
    aligned = shard // 8 * 8
    loads = []
    for m, (src, dst) in enumerate(((head_hbm, head), (embed_hbm, embed))):
        dst[whole:, :] = jnp.zeros((padded - whole, dst.shape[1]), dst.dtype)
        spans = [(0, aligned)] + [(aligned, shard - aligned)] * (shard > aligned)
        loads.append([
            torus.local(src.at[pl.ds(*span), :], dst.at[pl.ds(*span), :], load_sem.at[3 + m, i])
            for i, span in enumerate(spans)
        ])

    arrived(copies_h)
    copies_h = torus.gather_next(1, h_all, h_sems)
    arrived(copies_h)
    copies_h = torus.gather_next(2, h_all, h_sems)
    arrived(copies_x)
    copies_x = torus.gather_next(1, x_all, x_sems)
    arrived(weights)
    arrived(copies_h)
    arrived(copies_x)
    straight = torus.gather_last(x_all, x_sems, 0)

    hidden = h_all[...].reshape(rows, h_all.shape[-1]).astype(jnp.float32)
    mlp_in = rms_scale(hidden, mlp_gain_ref[...]).astype(jnp.bfloat16)
    gated = jnp.dot(mlp_in, gate[...], preferred_element_type=jnp.float32)
    upper = jnp.dot(mlp_in, up[...], preferred_element_type=jnp.float32)
    inner = (gated / (1.0 + jnp.exp(-gated)) * upper).astype(jnp.bfloat16)
    partial = jnp.dot(inner, down[...], preferred_element_type=jnp.float32)
    branch[...] = partial.astype(branch.dtype).reshape(branch.shape)
    relayed = []

    def pass_on(s):
        if s == 1:
            relayed.extend(torus.gather_last(x_all, x_sems, 1, straight))

    torus.reduce_scatter(branch, branch_buffers, summed, pass_on)

    final = resid_ref[...].astype(jnp.float32) + summed[...]
    last[...] = rms_scale(final, last_gain_ref[...]).astype(last.dtype)

    def exchange(m, j):
        part, got = ((part_e, got_e), (part_a, got_a))[m]
        return pltpu.make_async_remote_copy(
            src_ref=part.at[j, pl.ds(peer * rows, rows), :],
            dst_ref=got.at[j],
            send_sem=swap_send.at[m, j],
            recv_sem=swap_recv.at[m, j],
            device_id={"grp": peer, "voc": voc},
            device_id_type=MESH,
        )

    def partial_logits(m, first, stop):
        left, weight, part = ((x_all, head, part_e), (a_all, embed, part_a))[m]

        @pl.loop(first, stop)
        def _(j):
            block = weight[pl.ds(pl.multiple_of(j * TILE, TILE), TILE), :]
            part[j] = lax.dot_general(
                left[...].reshape(2 * rows, left.shape[-1]), block,
                (((1,), (1,)), ((), ())), preferred_element_type=jnp.float32,
            )
            exchange(m, j).start()

    copies_a = torus.gather_first(last, a_all, a_sems, True)
    arrived(relayed)
    arrived(loads[0])
    cut = (0, tiles // 4, tiles // 2, tiles)
    for s in range(1, 3):
        partial_logits(0, cut[s - 1], cut[s])
        arrived(copies_a)
        copies_a = torus.gather_next(s, a_all, a_sems)
    partial_logits(0, cut[2], cut[3])
    arrived(copies_a)
    arrived(loads[1])
    partial_logits(1, 0, tiles)

    picked[...] = jnp.zeros_like(picked)
    sums[...] = jnp.zeros_like(sums)
    target = jnp.broadcast_to(targ_ref[...], (LANES, rows)).T - voc * shard
    lane = lax.broadcasted_iota(jnp.int32, (rows, LANES), 1)
    slots = plaus_ref.shape[1] // LANES
    own = pl.ds(grp * rows, rows)

    @pl.loop(0, tiles)
    def _(j):
        exchange(0, j).wait()
        exchange(1, j).wait()
        for half in range(TILE // LANES):
            at = pl.ds(half * LANES, LANES)
            expert = part_e[j, own, at] + got_e[j, :, at]
            amateur = part_a[j, own, at] + got_a[j, :, at]
            chunk = j * (TILE // LANES) + half
            column = chunk * LANES + lane
            valid = column < shard
            sums[0] += jnp.where(valid, jnp.exp(expert), 0.0)
            sums[1] += jnp.where(valid, jnp.exp(amateur), 0.0)
            both = jnp.where(valid, expert - BETA * amateur, 0.0)
            sums[2] += jnp.where(column == target, both, 0.0)
            for s in range(slots):
                local = plaus_ref[:, s * LANES : (s + 1) * LANES] - voc * shard
                taken = jnp.take_along_axis(both, local & (LANES - 1), axis=1)
                here = (local >> 7 == chunk) & (local < shard)
                picked[s] = jnp.where(here, taken, picked[s])

    place = (*found.shape[:3], LANES)
    for s in range(slots):
        found[:, :, :, s * LANES : (s + 1) * LANES] = picked[s].reshape(place)
    total_e = jnp.sum(sums[0], axis=1, keepdims=True)
    total_a = jnp.sum(sums[1], axis=1, keepdims=True)
    at_target = jnp.sum(sums[2], axis=1, keepdims=True)
    tail = jnp.where(lane == 0, at_target, jnp.where(lane == 1, total_e, total_a))
    found[:, :, :, slots * LANES :] = tail.reshape(place)

    torus.reduce_scatter(found, found_buffers, total_ref, lambda s: torus.drain(AXES * (RING - 1)))
    count = slots * LANES
    total = total_ref[...]
    shift = jnp.log(total[:, count + 1 : count + 2]) - BETA * jnp.log(total[:, count + 2 : count + 3])
    scores = total[:, :count] - shift
    contrast = scores - jnp.log(jnp.sum(jnp.exp(scores), axis=1, keepdims=True))
    out_ref[...] = contrast
    entropy = -jnp.sum(jnp.exp(contrast) * contrast, axis=1, keepdims=True)
    lane = lax.broadcasted_iota(jnp.int32, stat_ref.shape, 1)
    stat_ref[...] = jnp.where(lane == 0, entropy, total[:, count : count + 1] - shift)
    torus.drain()


def on_device(
    expert_hidden,
    expert_gain,
    expert_head,
    amateur_hidden,
    mlp_gain,
    gate_weight,
    up_weight,
    down_weight,
    amateur_gain,
    amateur_embed,
    plausible,
    targets,
):
    rows, slots = plausible.shape
    shard, wide = expert_head.shape
    narrow = amateur_embed.shape[1]
    width, units = gate_weight.shape
    padded = pl.cdiv(shard, TILE) * TILE
    tiles = padded // TILE
    bf16, f32 = jnp.bfloat16, jnp.float32
    vmem = pl.BlockSpec(memory_space=pltpu.VMEM)
    hbm = pl.BlockSpec(memory_space=pl.ANY)
    dma = pltpu.SemaphoreType.DMA
    stage_sems = [dma((3, AXES, 2 * RING))] * 2
    torus_rows = (RING, RING, RING * OWN)
    out, stats = pl.pallas_call(
        whole_kernel,
        out_shape=(
            jax.ShapeDtypeStruct((OWN, slots), f32),
            jax.ShapeDtypeStruct((OWN, LANES), f32),
        ),
        in_specs=[vmem] * 7 + [hbm] * 5,
        out_specs=(vmem, vmem),
        scratch_shapes=[
            pltpu.VMEM((width, units), bf16),
            pltpu.VMEM((width, units), bf16),
            pltpu.VMEM((units, width), bf16),
            pltpu.VMEM((padded, wide), bf16),
            pltpu.VMEM((padded, narrow), bf16),
            dma((5, 2)),
            pltpu.VMEM((OWN, 2 * wide), bf16),
            pltpu.VMEM((2, *torus_rows, wide), bf16),
            stage_sems,
            pltpu.VMEM((1, *torus_rows, width), bf16),
            stage_sems,
            pltpu.VMEM((OWN, width), bf16),
            pltpu.VMEM((2, *torus_rows, narrow), bf16),
            stage_sems,
            pltpu.VMEM((*torus_rows, width), bf16),
            reduce_buffers(width, bf16),
            pltpu.VMEM((OWN, width), f32),
            pltpu.VMEM((tiles, 2 * rows, TILE), f32),
            pltpu.VMEM((tiles, 2 * rows, TILE), f32),
            pltpu.VMEM((tiles, rows, TILE), f32),
            pltpu.VMEM((tiles, rows, TILE), f32),
            pltpu.VMEM((slots // LANES, rows, LANES), f32),
            pltpu.VMEM((3, rows, LANES), f32),
            dma((2, tiles)),
            dma((2, tiles)),
            pltpu.VMEM((*torus_rows, slots + LANES), f32),
            reduce_buffers(slots + LANES, f32),
            pltpu.VMEM((OWN, slots + LANES), f32),
        ],
        compiler_params=pltpu.CompilerParams(
            collective_id=0, has_side_effects=True, vmem_limit_bytes=60 << 20
        ),
    )(
        expert_hidden, expert_gain[None], amateur_hidden, mlp_gain[None], amateur_gain[None],
        plausible, targets[None], gate_weight, up_weight, down_weight, expert_head, amateur_embed,
    )
    return (out, stats[:, 0], stats[:, 1])


def solution(mesh):
    in_specs = (
        P(("grp", "voc"), None),
        P(),
        P("voc", "grp"),
        P(("grp", "voc"), None),
        P(),
        P(None, "voc"),
        P(None, "voc"),
        P("voc", None),
        P(),
        P("voc", "grp"),
        P("grp", None),
        P("grp"),
    )
    out_specs = (P(("grp", "voc"), None), P(("grp", "voc")), P(("grp", "voc")))
    return jax.shard_map(
        on_device, mesh=mesh, in_specs=in_specs, out_specs=out_specs, check_vma=False
    )
```
